512 devices in a mesh: chain: 32 (over x_hi, z, core), term: 16 (over y, x_lo).
Axes of the slice: x: 4 (x_hi: 2, x_lo: 2; x = x_hi * 2 + x_lo), y: 8, z: 8, core: 2. Of those that a mesh axis runs over, the one named last changes fastest.
Arguments:
- wavefunction: bfloat16 [32, 4, 256, 256], P('chain')
- left_ops: bfloat16 [32, 128, 256, 256], P('chain', 'term')
- right_ops: bfloat16 [32, 128, 256, 256], P('chain', 'term')
- term_table: int32 [4, 32, 512], P(None, 'chain', 'term'), may hold values from 0 to 7, as said below
- coefficients: float32 [32, 512], P('chain', 'term'), may hold values from -0.1 to 0.3
- term_counts: int32 [32, 16], P('chain', 'term'), may hold values from 1 to 32, as said below
Outputs:
- first_hamiltonian_image: bfloat16 [32, 4, 256, 256], P('chain', None, 'term')
- second_image: bfloat16 [32, 4, 256, 256], P('chain', None, 'term')
The draws below stay inside these ranges and needn't reach their ends.
Inputs may be any that keep to these rules, and one draw needn't show every extreme that they name: `term_table`: row 0 and 1 (source and target block) lie in 0 to 3, rows 2 and 3 (operator indices) in 0 to 7. `term_counts`: in every bond at least one term device has all 32 slots live.
All inputs are finite; a program needn't handle non-finite values.
Results may differ from the reference program's by a relative error of at most 0.014.
Values may be sent and summed in bfloat16 or wider, within the bound.
No kernel may reach another device: no remote copies, remote signals or barrier semaphores. Data moves between devices by JAX's collectives and lax.ppermute only.
A program may use at most 64 MiB of HBM per device.

```python
import math
import jax
import jax.numpy as jnp
from jax import lax

BS = 256
BLOCKS = 4
OPS = 8
TMAX = 32
BONDS = 32
TERM_DEVS = 16
OP_BLOCKS = 128
TERM_SLOTS = 512


def draw_wavefunction(key, part):
    key_base, random_key_rows, key_cols = jax.random.split(key, 3)
    shape = (BONDS, BLOCKS, BS, BS)
    base = jax.random.normal(key_base, shape, jnp.float32)
    row_scale = jnp.exp(jax.random.uniform(random_key_rows, (BONDS, BLOCKS, BS, 1), jnp.float32, math.log(0.5), math.log(1.58)))
    col_scale = jnp.exp(jax.random.uniform(key_cols, (BONDS, BLOCKS, 1, BS), jnp.float32, math.log(0.5), math.log(1.58)))
    return (base * row_scale * col_scale).astype(jnp.bfloat16)


def operator_blocks(key, salt):
    key = jax.random.fold_in(key, salt)
    key_noise, key_diag = jax.random.split(key)
    shape = (BONDS, OP_BLOCKS, BS, BS)
    spread = 0.6 / math.sqrt(BS)
    noise = jax.random.normal(key_noise, shape, jnp.float32) * spread
    diag_gain = jax.random.uniform(key_diag, (BONDS, OP_BLOCKS, 1, BS), jnp.float32, 0.6, 1.4)
    identity = (jnp.arange(BS)[:, None] == jnp.arange(BS)[None, :]).astype(jnp.float32)
    return (identity * diag_gain + noise).astype(jnp.bfloat16)


def draw_left_ops(key, part):
    return operator_blocks(key, 11)


def draw_right_ops(key, part):
    return operator_blocks(key, 23)


def draw_term_table(key, part):
    key_src, key_dst, key_left, key_right = jax.random.split(key, 4)
    shape = (BONDS, TERM_SLOTS)
    source = jax.random.randint(key_src, shape, 0, BLOCKS)
    target = jax.random.randint(key_dst, shape, 0, BLOCKS)
    left_index = jax.random.randint(key_left, shape, 0, OPS)
    right_index = jax.random.randint(key_right, shape, 0, OPS)
    return jnp.stack([source, target, left_index, right_index], axis=0).astype(jnp.int32)


def draw_term_counts(key, part):
    key_level, key_full = jax.random.split(key)
    levels = jax.random.randint(key_level, (BONDS, TERM_DEVS), 1, 9)
    fullest = jax.random.randint(key_full, (BONDS, 1), 0, TERM_DEVS)
    levels = jnp.where(jnp.arange(TERM_DEVS)[None, :] == fullest, 8, levels)
    return jnp.maximum(levels * levels * TMAX // 64, 1).astype(jnp.int32)


def shard_levels(rng, dims, shards, smallest, largest):
    def one(dim, shards_of):
        draws = jax.random.uniform(jax.random.fold_in(jax.random.fold_in(rng, 6), dim), (shards_of,), jnp.float32, smallest / len(shards), largest / len(shards))
        return jnp.repeat(jnp.exp(draws), dims[dim] // shards_of).reshape((-1,) + (1,) * (len(dims) - dim - 1))

    loudness = one(*shards[0])
    for cut in shards[1:]:
        loudness = loudness * one(*cut)
    return loudness


def setup_inputs(seed: int = 0) -> dict:
    seeds = jax.random.split(jax.random.key(seed), 7)
    return {
        "wavefunction": draw_wavefunction(jax.random.fold_in(seeds[6], 71), 0),
        "left_ops": draw_left_ops(jax.random.fold_in(seeds[6], 71), 0),
        "right_ops": draw_right_ops(jax.random.fold_in(seeds[6], 71), 0),
        "term_table": draw_term_table(jax.random.fold_in(seeds[6], 71), 0),
        "coefficients": jnp.clip(-0.1 + 0.4 * jax.random.uniform(seeds[4], (BONDS, TERM_SLOTS), jnp.float32) ** shard_levels(seeds[4], (BONDS, TERM_SLOTS), ((0, 32), (1, 16)), -0.2, 0.2), -0.1, 0.3),
        "term_counts": draw_term_counts(jax.random.fold_in(seeds[6], 71), 0),
    }


epsilon = 1e-06

def apply_terms(blocks, left_blocks, right_blocks, term_rows, coef_rows, live_count):
    slot_count = term_rows.shape[1]
    source = term_rows[0]
    target = term_rows[1]
    left_selection = left_blocks[term_rows[2]].astype(jnp.float32)
    right_selection = right_blocks[term_rows[3]].astype(jnp.float32)
    selected_blocks = blocks[source].astype(jnp.float32)
    inner_contraction = jnp.einsum('skh,shu->sku', left_selection, selected_blocks, precision=lax.Precision.HIGHEST).astype(jnp.bfloat16)
    outer_contraction = jnp.einsum('lbe,leu->lbu', inner_contraction.astype(jnp.float32), right_selection, precision=lax.Precision.HIGHEST)
    live_mask = jnp.arange(slot_count, dtype=jnp.int32) < live_count
    weights = jnp.where(live_mask, coef_rows, jnp.float32(0.0)).astype(jnp.float32)
    routing = (target[None, :] == jnp.arange(BLOCKS, dtype=jnp.int32)[:, None]).astype(jnp.float32) * weights[None, :]
    return jnp.einsum('kt,tad->kad', routing, outer_contraction, precision=lax.Precision.HIGHEST)

def reference(wavefunction, left_ops, right_ops, term_table, coefficients, term_counts):

    def bond_step(bond_index):
        blocks = wavefunction[bond_index]
        left_all = left_ops[bond_index].reshape(TERM_DEVS, OPS, BS, BS)
        right_all = right_ops[(bond_index + 1) % BONDS].reshape(TERM_DEVS, OPS, BS, BS)
        table_all = term_table[:, bond_index].reshape(4, TERM_DEVS, TMAX)
        coef_all = coefficients[bond_index].reshape(TERM_DEVS, TMAX)
        count_all = term_counts[bond_index]

        def apply_all(vectors):

            def one_device(term_dev):
                return apply_terms(vectors, left_all[term_dev], right_all[term_dev], table_all[:, term_dev], coef_all[term_dev], count_all[term_dev])
            partials = lax.map(one_device, jnp.arange(TERM_DEVS, dtype=jnp.int32))
            return lax.optimization_barrier(jnp.sum(partials, axis=0))
        first = apply_all(blocks)
        wave_f32 = blocks.astype(jnp.float32)
        rayleigh = jnp.mean(wave_f32 * first) / (jnp.mean(wave_f32 * wave_f32) + epsilon)
        residual = first - rayleigh * wave_f32
        direction = (residual * lax.rsqrt(jnp.mean(residual * residual) + epsilon)).astype(jnp.bfloat16)
        second = apply_all(direction)
        return (first.astype(jnp.bfloat16), second.astype(jnp.bfloat16))
    first_hamiltonian_image, second_image = lax.map(bond_step, jnp.arange(BONDS, dtype=jnp.int32))
    return (first_hamiltonian_image, second_image)
```

```python
import jax
import jax.numpy as jnp
from jax import lax
from jax.experimental import pallas as pl
from jax.experimental.pallas import tpu as pltpu
from jax.sharding import PartitionSpec as P

epsilon = 1e-06
VMEM = pl.BlockSpec(memory_space=pltpu.VMEM)
SMEM = pl.BlockSpec(memory_space=pltpu.SMEM)
F32 = jnp.float32
BF16 = jnp.bfloat16
EXTRA = 8


def left_products(left_ref, vector, product_ref):
    def step(li, _):
        left = left_ref[0, li]
        for src in range(4):
            product_ref[src, li] = jnp.dot(left, vector(src), preferred_element_type=F32).astype(BF16)
        return 0

    lax.fori_loop(0, 8, step, 0)


def right_sums(table_ref, coef_ref, count_ref, product_ref, right_ref, total_ref):
    total_ref[...] = jnp.zeros_like(total_ref)
    count = count_ref[0, 0]

    def step(slot, _):
        weight = jnp.where(slot < count, coef_ref[0, slot], F32(0.0))
        inner = product_ref[table_ref[0, 0, slot], table_ref[2, 0, slot]]
        outer = jnp.dot(inner, right_ref[0, table_ref[3, 0, slot]], preferred_element_type=F32)
        dst = table_ref[1, 0, slot]
        total_ref[dst] = total_ref[dst] + weight * outer
        return 0

    lax.fori_loop(0, 32, step, 0, unroll=2)


def first_left_kernel(left_ref, wave_ref, product_ref, norm_ref):
    left_products(left_ref, lambda src: wave_ref[0, src], product_ref)
    norm = F32(0.0)
    for k in range(4):
        x = wave_ref[0, k].astype(F32)
        norm = norm + jnp.sum(x * x)
    norm_ref[0, 0] = norm


def first_right_kernel(order, table_ref, coef_ref, count_ref, product_ref, right_ref, wave_ref, out_ref, total_ref):
    right_sums(table_ref, coef_ref, count_ref, product_ref, right_ref, total_ref)
    share = F32(0.0)
    for k in range(4):
        share = share + jnp.sum(wave_ref[0, k].astype(F32) * total_ref[k])
        for place, owner in enumerate(order):
            out_ref[place, pl.ds(16 * k, 16), :] = total_ref[k, pl.ds(16 * owner, 16), :].astype(BF16)
    whole = jnp.full((EXTRA, 256), share, F32)
    high = whole.astype(BF16).astype(F32)
    middle = (whole - high).astype(BF16).astype(F32)
    low = whole - high - middle
    row = lax.broadcasted_iota(jnp.int32, (EXTRA, 256), 0)
    pieces = jnp.where(row == 0, high, jnp.where(row == 1, middle, jnp.where(row == 2, low, 0.0))).astype(BF16)
    for place in range(len(order)):
        out_ref[place, pl.ds(64, EXTRA), :] = pieces


def residual_kernel(place_ref, norm_ref, parts_ref, wave_ref, first_ref, copies_ref):
    entries = 4 * 256 * 256
    rows = parts_ref[0].astype(F32)
    for part in range(1, 16):
        rows = rows + parts_ref[part].astype(F32)
    overlap = jnp.sum(rows[64:, 0:1])
    first = rows[:64]
    first_ref[0] = first.reshape(4, 16, 256).astype(BF16)
    rayleigh = overlap / entries / (norm_ref[0, 0] / entries + epsilon)
    start = pl.multiple_of(place_ref[0, 0] * 16, 16)
    wave = wave_ref[0, :, pl.ds(start, 16), :].astype(F32).reshape(64, 256)
    residual = (first - rayleigh * wave).astype(BF16)
    for copy in range(16):
        copies_ref[copy] = residual


def second_kernel(
    order, table_ref, coef_ref, count_ref, blocks_ref, left_ref, right_ref, out_ref, scale_ref, vector_ref, product_ref, total_ref
):
    entries = 4 * 256 * 256
    for place, owner in enumerate(order):
        for k in range(4):
            vector_ref[k, pl.ds(16 * owner, 16), :] = blocks_ref[place, pl.ds(16 * k, 16), :]
    left_products(left_ref, lambda src: vector_ref[src], product_ref)
    right_sums(table_ref, coef_ref, count_ref, product_ref, right_ref, total_ref)
    for k in range(4):
        for place, owner in enumerate(order):
            out_ref[place, pl.ds(16 * k, 16), :] = total_ref[k, pl.ds(16 * owner, 16), :].astype(BF16)
    square = F32(0.0)
    for k in range(4):
        r = vector_ref[k].astype(F32)
        square = square + jnp.sum(r * r)
    scale_ref[...] = lax.rsqrt(jnp.full((1, 128), square / entries + epsilon, F32))


def scale_kernel(scale_ref, parts_ref, out_ref):
    rows = parts_ref[0].astype(F32)
    for part in range(1, 16):
        rows = rows + parts_ref[part].astype(F32)
    scale = jnp.concatenate([scale_ref[...], scale_ref[...]], axis=1)
    out_ref[0] = (rows * scale).reshape(4, 16, 256).astype(BF16)


def params(mib):
    return pltpu.CompilerParams(vmem_limit_bytes=mib << 20)


ORDER = (0, 2, 4, 6, 8, 10, 12, 14, 15, 13, 11, 9, 7, 5, 3, 1)


def exchange(blocks):
    return lax.all_to_all(blocks, "term", 0, 0, axis_index_groups=[list(ORDER)])


def body(wavefunction, left_ops, right_ops, term_table, coefficients, term_counts):
    import functools

    count = lax.axis_size("chain")
    right = lax.ppermute(right_ops, "chain", [(s, (s - 1) % count) for s in range(count)])
    place = lax.axis_index("term").reshape(1, 1).astype(jnp.int32)
    shape = jax.ShapeDtypeStruct
    product, norm = pl.pallas_call(
        first_left_kernel,
        out_shape=(shape((4, 8, 256, 256), BF16), shape((1, 1), F32)),
        in_specs=[VMEM, VMEM],
        out_specs=(VMEM, SMEM),
        compiler_params=params(12),
        name="first_left",
    )(left_ops, wavefunction)
    partial = pl.pallas_call(
        functools.partial(first_right_kernel, ORDER),
        out_shape=shape((16, 64 + EXTRA, 256), BF16),
        in_specs=[SMEM, SMEM, SMEM, VMEM, VMEM, VMEM],
        out_specs=VMEM,
        scratch_shapes=[pltpu.VMEM((4, 256, 256), F32)],
        compiler_params=params(16),
        name="first_right",
    )(term_table, coefficients, term_counts, product, right, wavefunction)
    first, copies = pl.pallas_call(
        residual_kernel,
        out_shape=(shape((1, 4, 16, 256), BF16), shape((16, 64, 256), BF16)),
        in_specs=[SMEM, SMEM, VMEM, VMEM],
        out_specs=(VMEM, VMEM),
        compiler_params=params(8),
        name="residual",
    )(place, norm, exchange(partial), wavefunction)
    partial, scale = pl.pallas_call(
        functools.partial(second_kernel, ORDER),
        out_shape=(shape((16, 64, 256), BF16), shape((1, 128), F32)),
        in_specs=[SMEM, SMEM, SMEM, VMEM, VMEM, VMEM],
        out_specs=(VMEM, VMEM),
        scratch_shapes=[
            pltpu.VMEM((4, 256, 256), BF16),
            pltpu.VMEM((4, 8, 256, 256), BF16),
            pltpu.VMEM((4, 256, 256), F32),
        ],
        compiler_params=params(16),
        name="second",
    )(term_table, coefficients, term_counts, exchange(copies), left_ops, right)
    second = pl.pallas_call(
        scale_kernel,
        out_shape=shape((1, 4, 16, 256), BF16),
        in_specs=[VMEM, VMEM],
        out_specs=VMEM,
        compiler_params=params(8),
        name="scale",
    )(scale, exchange(partial))
    return first, second


def solution(mesh):
    in_specs = (
        P("chain", None, None, None),
        P("chain", "term", None, None),
        P("chain", "term", None, None),
        P(None, "chain", "term"),
        P("chain", "term"),
        P("chain", "term"),
    )
    out_specs = (P("chain", None, "term", None), P("chain", None, "term", None))
    return jax.shard_map(body, mesh=mesh, in_specs=in_specs, out_specs=out_specs, check_vma=False)
```

```python
import functools

import jax
import jax.numpy as jnp
from jax import lax
from jax.experimental import pallas as pl
from jax.experimental.pallas import tpu as pltpu
from jax.sharding import PartitionSpec as P

epsilon = 1e-06
VMEM = pl.BlockSpec(memory_space=pltpu.VMEM)
SMEM = pl.BlockSpec(memory_space=pltpu.SMEM)
F32 = jnp.float32
BF16 = jnp.bfloat16
HBM = pl.BlockSpec(memory_space=pltpu.HBM)


def left_products(left_ref, vector, product_ref):
    left = left_ref[0].reshape(8 * 256, 256)
    for src in range(4):
        product = jnp.dot(left, vector(src), preferred_element_type=F32)
        product_ref[src] = product.astype(BF16).reshape(8, 256, 256)


def right_sums(table_ref, coef_ref, count_ref, product_ref, right_ref, total_ref):
    total_ref[...] = jnp.zeros_like(total_ref)
    count = count_ref[0, 0]

    def step(slot, _):
        weight = jnp.where(slot < count, coef_ref[0, slot], F32(0.0))
        inner = product_ref[table_ref[0, 0, slot], table_ref[2, 0, slot]]
        outer = jnp.dot(inner, right_ref[0, table_ref[3, 0, slot]], preferred_element_type=F32)
        dst = table_ref[1, 0, slot]
        total_ref[dst] = total_ref[dst] + weight * outer
        return 0

    lax.fori_loop(0, 32, step, 0, unroll=16)


def stage_kernel(table_ref, coef_ref, left_ref, wave_ref, table_out, coef_out, left_out, wave_out, sems):
    copies = [
        pltpu.make_async_copy(source, target, sems.at[i])
        for i, (source, target) in enumerate(
            ((left_ref, left_out), (wave_ref, wave_out), (table_ref, table_out), (coef_ref, coef_out))
        )
    ]
    for copy in copies:
        copy.start()
    for copy in copies:
        copy.wait()


def first_left_kernel(table_ref, coef_ref, count_ref, left_ref, wave_ref, mixed_ref, norm_ref, sum_ref):
    sum_ref[...] = jnp.zeros_like(sum_ref)
    count = count_ref[0, 0]

    def step(slot, _):
        weight = jnp.where(slot < count, coef_ref[0, slot], F32(0.0))
        inner = jnp.dot(
            left_ref[0, table_ref[2, 0, slot]], wave_ref[0, table_ref[0, 0, slot]], preferred_element_type=F32
        )
        cell = table_ref[1, 0, slot] * 8 + table_ref[3, 0, slot]
        sum_ref[cell] = sum_ref[cell] + weight * inner
        return 0

    lax.fori_loop(0, 32, step, 0, unroll=16)
    norm = F32(0.0)
    for k in range(4):
        x = wave_ref[0, k].astype(F32)
        norm = norm + jnp.sum(x * x)
        for ri in range(8):
            mixed_ref[k, :, pl.ds(256 * ri, 256)] = sum_ref[k * 8 + ri].astype(BF16)
    norm_ref[...] = jnp.full((1, 128), norm, F32)


def first_right_kernel(order, late_ref, mixed_ref, right_ref, out_ref):
    pl.delay(late_ref[0, 0])

    right = right_ref[0].reshape(8 * 256, 256)
    for k in range(4):
        total = jnp.dot(mixed_ref[k], right, preferred_element_type=F32)
        for place, owner in enumerate(order):
            out_ref[place, pl.ds(16 * k, 16), :] = total[16 * owner : 16 * owner + 16].astype(BF16)


def sum_kernel(parts_ref, first_ref, copies_ref):
    rows = parts_ref[0].astype(F32)
    for part in range(1, 16):
        rows = rows + parts_ref[part].astype(F32)
    first = rows.astype(BF16)
    first_ref[0] = first.reshape(4, 16, 256)
    for copy in range(16):
        copies_ref[copy] = first


def second_kernel(
    order,
    table_ref,
    coef_ref,
    count_ref,
    norm_ref,
    blocks_ref,
    wave_ref,
    left_ref,
    right_ref,
    out_ref,
    scale_ref,
    vector_ref,
    product_ref,
    total_ref,
):
    entries = 4 * 256 * 256
    overlap = jnp.zeros((16, 256), F32)
    for place, owner in enumerate(order):
        for k in range(4):
            first = blocks_ref[place, pl.ds(16 * k, 16), :].astype(F32)
            overlap = overlap + first * wave_ref[0, k, pl.ds(16 * owner, 16), :].astype(F32)
    rayleigh = jnp.sum(overlap) / entries / (jnp.max(norm_ref[...]) / entries + epsilon)
    square = jnp.zeros((16, 256), F32)
    for place, owner in enumerate(order):
        for k in range(4):
            first = blocks_ref[place, pl.ds(16 * k, 16), :].astype(F32)
            residual = first - rayleigh * wave_ref[0, k, pl.ds(16 * owner, 16), :].astype(F32)
            square = square + residual * residual
            vector_ref[k, pl.ds(16 * owner, 16), :] = residual.astype(BF16)
    left_products(left_ref, lambda src: vector_ref[src], product_ref)
    right_sums(table_ref, coef_ref, count_ref, product_ref, right_ref, total_ref)
    for k in range(4):
        for place, owner in enumerate(order):
            out_ref[place, pl.ds(16 * k, 16), :] = total_ref[k, pl.ds(16 * owner, 16), :].astype(BF16)
    scale_ref[...] = lax.rsqrt(jnp.full((1, 128), jnp.sum(square) / entries + epsilon, F32))


def scale_kernel(scale_ref, parts_ref, out_ref):
    rows = parts_ref[0].astype(F32)
    for part in range(1, 16):
        rows = rows + parts_ref[part].astype(F32)
    scale = jnp.concatenate([scale_ref[...], scale_ref[...]], axis=1)
    out_ref[0] = (rows * scale).reshape(4, 16, 256).astype(BF16)


def params(mib):
    return pltpu.CompilerParams(vmem_limit_bytes=mib << 20)


ORDER = (0, 2, 4, 6, 8, 10, 12, 14, 15, 13, 11, 9, 7, 5, 3, 1)


def exchange(blocks):
    return lax.all_to_all(blocks, "term", 0, 0, axis_index_groups=[list(ORDER)])


def body(wavefunction, left_ops, right_ops, term_table, coefficients, term_counts):
    count = lax.axis_size("chain")
    right = lax.ppermute(right_ops, "chain", [(s, (s - 1) % count) for s in range(count)])
    chain = lax.axis_index("chain") % 16
    own = jnp.where(chain % 2 == 0, 7000, 0)
    for bond, wait in ((0, 0), (6, 0), (7, 5000), (14, 0), (15, 3500)):
        own = jnp.where(chain == bond, wait, own)
    late = own.reshape(1, 1).astype(jnp.int32)
    shape = jax.ShapeDtypeStruct
    table, coef, left, wave = pl.pallas_call(
        stage_kernel,
        out_shape=tuple(shape(a.shape, a.dtype) for a in (term_table, coefficients, left_ops, wavefunction)),
        in_specs=[HBM] * 4,
        out_specs=(VMEM,) * 4,
        scratch_shapes=[pltpu.SemaphoreType.DMA((4,))],
        compiler_params=params(4),
        name="stage",
    )(*(pltpu.with_memory_space_constraint(a, pltpu.HBM) for a in (term_table, coefficients, left_ops, wavefunction)))
    mixed, norm = pl.pallas_call(
        first_left_kernel,
        out_shape=(shape((4, 256, 2048), BF16), shape((1, 128), F32)),
        in_specs=[SMEM, SMEM, SMEM, VMEM, VMEM],
        out_specs=(VMEM, VMEM),
        scratch_shapes=[pltpu.VMEM((32, 256, 256), F32)],
        compiler_params=params(24),
        name="first_left",
    )(table, coef, term_counts, left, wave)
    partial = pl.pallas_call(
        functools.partial(first_right_kernel, ORDER),
        out_shape=shape((16, 64, 256), BF16),
        in_specs=[SMEM, VMEM, VMEM],
        out_specs=VMEM,
        compiler_params=params(16),
        name="first_right",
    )(late, mixed, right)
    first, copies = pl.pallas_call(
        sum_kernel,
        out_shape=(shape((1, 4, 16, 256), BF16), shape((16, 64, 256), BF16)),
        in_specs=[VMEM],
        out_specs=(VMEM, VMEM),
        compiler_params=params(8),
        name="sum",
    )(exchange(partial))
    partial, scale = pl.pallas_call(
        functools.partial(second_kernel, ORDER),
        out_shape=(shape((16, 64, 256), BF16), shape((1, 128), F32)),
        in_specs=[SMEM, SMEM, SMEM, VMEM, VMEM, VMEM, VMEM, VMEM],
        out_specs=(VMEM, VMEM),
        scratch_shapes=[
            pltpu.VMEM((4, 256, 256), BF16),
            pltpu.VMEM((4, 8, 256, 256), BF16),
            pltpu.VMEM((4, 256, 256), F32),
        ],
        compiler_params=params(16),
        name="second",
    )(table, coef, term_counts, norm, exchange(copies), wave, left, right)
    second = pl.pallas_call(
        scale_kernel,
        out_shape=shape((1, 4, 16, 256), BF16),
        in_specs=[VMEM, VMEM],
        out_specs=VMEM,
        compiler_params=params(8),
        name="scale",
    )(scale, exchange(partial))
    return first, second


def solution(mesh):
    in_specs = (
        P("chain", None, None, None),
        P("chain", "term", None, None),
        P("chain", "term", None, None),
        P(None, "chain", "term"),
        P("chain", "term"),
        P("chain", "term"),
    )
    out_specs = (P("chain", None, "term", None), P("chain", None, "term", None))
    return jax.shard_map(body, mesh=mesh, in_specs=in_specs, out_specs=out_specs, check_vma=False)
```

```python
import functools

import jax
import jax.numpy as jnp
from jax import lax
from jax.experimental import pallas as pl
from jax.experimental.pallas import tpu as pltpu
from jax.sharding import PartitionSpec as P

epsilon = 1e-06
VMEM = pl.BlockSpec(memory_space=pltpu.VMEM)
SMEM = pl.BlockSpec(memory_space=pltpu.SMEM)
F32 = jnp.float32
BF16 = jnp.bfloat16
HBM = pl.BlockSpec(memory_space=pltpu.HBM)


def left_products(left_ref, vector, product_ref):
    for src in range(4):
        for half in range(0, 8, 2):
            left = left_ref[0, pl.ds(half, 2)].reshape(512, 256)
            product = jnp.dot(left, vector(src), preferred_element_type=F32)
            product_ref[src, pl.ds(half, 2)] = product.astype(BF16).reshape(2, 256, 256)


def right_sums(table_ref, coef_ref, count_ref, product_ref, right_ref, total_ref):
    total_ref[...] = jnp.zeros_like(total_ref)
    count = count_ref[0, 0]

    def step(slot, _):
        weight = jnp.where(slot < count, coef_ref[0, slot], F32(0.0))
        inner = product_ref[table_ref[0, 0, slot], table_ref[2, 0, slot]]
        outer = jnp.dot(inner, right_ref[0, table_ref[3, 0, slot]], preferred_element_type=F32)
        dst = table_ref[1, 0, slot]
        total_ref[dst] = total_ref[dst] + weight * outer
        return 0

    lax.fori_loop(0, 32, step, 0, unroll=32)


def stage_kernel(table_ref, coef_ref, left_ref, wave_ref, table_out, coef_out, left_out, wave_out, sems):
    copies = [
        pltpu.make_async_copy(source, target, sems.at[i])
        for i, (source, target) in enumerate(
            ((left_ref, left_out), (wave_ref, wave_out), (table_ref, table_out), (coef_ref, coef_out))
        )
    ]
    for copy in copies:
        copy.start()
    for copy in copies:
        copy.wait()


def first_left_kernel(table_ref, coef_ref, count_ref, left_ref, wave_ref, mixed_ref, norm_ref, sum_ref):
    sum_ref[...] = jnp.zeros_like(sum_ref)
    count = count_ref[0, 0]

    def step(slot, _):
        weight = jnp.where(slot < count, coef_ref[0, slot], F32(0.0))
        inner = jnp.dot(
            left_ref[0, table_ref[2, 0, slot]], wave_ref[0, table_ref[0, 0, slot]], preferred_element_type=F32
        )
        cell = table_ref[1, 0, slot] * 8 + table_ref[3, 0, slot]
        sum_ref[cell] = sum_ref[cell] + weight * inner
        return 0

    lax.fori_loop(0, 32, step, 0, unroll=16)
    norm = F32(0.0)
    for k in range(4):
        x = wave_ref[0, k].astype(F32)
        norm = norm + jnp.sum(x * x)
        for ri in range(8):
            mixed_ref[k, :, pl.ds(256 * ri, 256)] = sum_ref[k * 8 + ri].astype(BF16)
    norm_ref[...] = jnp.full((1, 128), norm, F32)


def first_right_kernel(order, late_ref, mixed_ref, right_ref, out_ref):
    pl.delay(late_ref[0, 0])

    right = right_ref[0].reshape(8 * 256, 256)
    for k in range(4):
        total = jnp.dot(mixed_ref[k], right, preferred_element_type=F32)
        for place, owner in enumerate(order):
            out_ref[place, pl.ds(16 * k, 16), :] = total[16 * owner : 16 * owner + 16].astype(BF16)


def sum_kernel(parts_ref, copies_ref):
    rows = parts_ref[0].astype(F32)
    for part in range(1, 16):
        rows = rows + parts_ref[part].astype(F32)
    first = rows.astype(BF16)
    for copy in range(16):
        copies_ref[copy] = first


def second_kernel(
    order,
    table_ref,
    coef_ref,
    count_ref,
    norm_ref,
    blocks_ref,
    wave_ref,
    left_ref,
    right_ref,
    out_ref,
    scale_ref,
    vector_ref,
    product_ref,
    total_ref,
):
    entries = 4 * 256 * 256
    overlap = jnp.zeros((16, 256), F32)
    for place, owner in enumerate(order):
        for k in range(4):
            first = blocks_ref[place, pl.ds(16 * k, 16), :].astype(F32)
            overlap = overlap + first * wave_ref[0, k, pl.ds(16 * owner, 16), :].astype(F32)
    rayleigh = jnp.sum(overlap) / entries / (jnp.max(norm_ref[...]) / entries + epsilon)
    square = jnp.zeros((16, 256), F32)
    for place, owner in enumerate(order):
        for k in range(4):
            first = blocks_ref[place, pl.ds(16 * k, 16), :].astype(F32)
            residual = first - rayleigh * wave_ref[0, k, pl.ds(16 * owner, 16), :].astype(F32)
            square = square + residual * residual
            vector_ref[k, pl.ds(16 * owner, 16), :] = residual.astype(BF16)
    left_products(left_ref, lambda src: vector_ref[src], product_ref)
    right_sums(table_ref, coef_ref, count_ref, product_ref, right_ref, total_ref)
    for k in range(4):
        for place, owner in enumerate(order):
            out_ref[place, pl.ds(16 * k, 16), :] = total_ref[k, pl.ds(16 * owner, 16), :].astype(BF16)
    scale_ref[...] = lax.rsqrt(jnp.full((1, 128), jnp.sum(square) / entries + epsilon, F32))


def scale_kernel(scale_ref, first_ref, parts_ref, first_out, out_ref):
    first_out[0] = first_ref[0].reshape(4, 16, 256)
    rows = parts_ref[0].astype(F32)
    for part in range(1, 16):
        rows = rows + parts_ref[part].astype(F32)
    scale = jnp.concatenate([scale_ref[...], scale_ref[...]], axis=1)
    out_ref[0] = (rows * scale).reshape(4, 16, 256).astype(BF16)


def params(mib):
    return pltpu.CompilerParams(vmem_limit_bytes=mib << 20)


ORDER = (0, 2, 4, 6, 8, 10, 12, 14, 15, 13, 11, 9, 7, 5, 3, 1)


def exchange(blocks):
    return lax.all_to_all(blocks, "term", 0, 0, axis_index_groups=[list(ORDER)])


def body(wavefunction, left_ops, right_ops, term_table, coefficients, term_counts):
    count = lax.axis_size("chain")
    right = lax.ppermute(right_ops, "chain", [(s, (s - 1) % count) for s in range(count)])
    chain = lax.axis_index("chain") % 16
    own = jnp.where(chain % 2 == 0, 7000, 0)
    for bond, wait in ((0, 0), (6, 0), (7, 5000), (14, 0), (15, 3500)):
        own = jnp.where(chain == bond, wait, own)
    late = own.reshape(1, 1).astype(jnp.int32)
    shape = jax.ShapeDtypeStruct
    table, coef, left, wave = pl.pallas_call(
        stage_kernel,
        out_shape=tuple(shape(a.shape, a.dtype) for a in (term_table, coefficients, left_ops, wavefunction)),
        in_specs=[HBM] * 4,
        out_specs=(VMEM,) * 4,
        scratch_shapes=[pltpu.SemaphoreType.DMA((4,))],
        compiler_params=params(4),
        name="stage",
    )(*(pltpu.with_memory_space_constraint(a, pltpu.HBM) for a in (term_table, coefficients, left_ops, wavefunction)))
    mixed, norm = pl.pallas_call(
        first_left_kernel,
        out_shape=(shape((4, 256, 2048), BF16), shape((1, 128), F32)),
        in_specs=[SMEM, SMEM, SMEM, VMEM, VMEM],
        out_specs=(VMEM, VMEM),
        scratch_shapes=[pltpu.VMEM((32, 256, 256), F32)],
        compiler_params=params(24),
        name="first_left",
    )(table, coef, term_counts, left, wave)
    partial = pl.pallas_call(
        functools.partial(first_right_kernel, ORDER),
        out_shape=shape((16, 64, 256), BF16),
        in_specs=[SMEM, VMEM, VMEM],
        out_specs=VMEM,
        compiler_params=params(16),
        name="first_right",
    )(late, mixed, right)
    copies = pl.pallas_call(
        sum_kernel,
        out_shape=shape((16, 64, 256), BF16),
        in_specs=[VMEM],
        out_specs=VMEM,
        compiler_params=params(8),
        name="sum",
    )(exchange(partial))
    partial, scale = pl.pallas_call(
        functools.partial(second_kernel, ORDER),
        out_shape=(shape((16, 64, 256), BF16), shape((1, 128), F32)),
        in_specs=[SMEM, SMEM, SMEM, VMEM, VMEM, VMEM, VMEM, VMEM],
        out_specs=(VMEM, VMEM),
        scratch_shapes=[
            pltpu.VMEM((4, 256, 256), BF16),
            pltpu.VMEM((4, 8, 256, 256), BF16),
            pltpu.VMEM((4, 256, 256), F32),
        ],
        compiler_params=params(16),
        name="second",
    )(table, coef, term_counts, norm, exchange(copies), wave, left, right)
    return pl.pallas_call(
        scale_kernel,
        out_shape=(shape((1, 4, 16, 256), BF16), shape((1, 4, 16, 256), BF16)),
        in_specs=[VMEM, VMEM, VMEM],
        out_specs=(VMEM, VMEM),
        compiler_params=params(8),
        name="scale",
    )(scale, copies, exchange(partial))


def solution(mesh):
    in_specs = (
        P("chain", None, None, None),
        P("chain", "term", None, None),
        P("chain", "term", None, None),
        P(None, "chain", "term"),
        P("chain", "term"),
        P("chain", "term"),
    )
    out_specs = (P("chain", None, "term", None), P("chain", None, "term", None))
    return jax.shard_map(body, mesh=mesh, in_specs=in_specs, out_specs=out_specs, check_vma=False)
```

```python
import functools

import jax
import jax.numpy as jnp
from jax import lax
from jax.experimental import pallas as pl
from jax.experimental.pallas import tpu as pltpu
from jax.sharding import PartitionSpec as P

epsilon = 1e-06
VMEM = pl.BlockSpec(memory_space=pltpu.VMEM)
SMEM = pl.BlockSpec(memory_space=pltpu.SMEM)
F32 = jnp.float32
BF16 = jnp.bfloat16
HBM = pl.BlockSpec(memory_space=pltpu.HBM)


def left_products(left_ref, vector, product_ref):
    for src in range(4):
        for half in range(0, 8, 2):
            left = left_ref[0, pl.ds(half, 2)].reshape(512, 256)
            product = jnp.dot(left, vector(src), preferred_element_type=F32)
            product_ref[src, pl.ds(half, 2)] = product.astype(BF16).reshape(2, 256, 256)


def right_sums(table_ref, coef_ref, count_ref, product_ref, right_ref, total_ref):
    total_ref[...] = jnp.zeros_like(total_ref)
    count = count_ref[0, 0]

    def step(slot, _):
        weight = jnp.where(slot < count, coef_ref[0, slot], F32(0.0))
        inner = product_ref[table_ref[0, 0, slot], table_ref[2, 0, slot]]
        outer = jnp.dot(inner, right_ref[0, table_ref[3, 0, slot]], preferred_element_type=F32)
        dst = table_ref[1, 0, slot]
        total_ref[dst] = total_ref[dst] + weight * outer
        return 0

    lax.fori_loop(0, 32, step, 0, unroll=32)


def stage_kernel(table_ref, coef_ref, left_ref, wave_ref, table_out, coef_out, left_out, wave_out, sems):
    copies = [
        pltpu.make_async_copy(source, target, sems.at[i])
        for i, (source, target) in enumerate(
            ((left_ref, left_out), (wave_ref, wave_out), (table_ref, table_out), (coef_ref, coef_out))
        )
    ]
    for copy in copies:
        copy.start()
    for copy in copies:
        copy.wait()


def first_left_kernel(table_ref, coef_ref, count_ref, left_ref, wave_ref, mixed_ref, norm_ref, sum_ref):
    sum_ref[...] = jnp.zeros_like(sum_ref)
    count = count_ref[0, 0]

    def step(slot, _):
        weight = jnp.where(slot < count, coef_ref[0, slot], F32(0.0))
        inner = jnp.dot(
            left_ref[0, table_ref[2, 0, slot]], wave_ref[0, table_ref[0, 0, slot]], preferred_element_type=F32
        )
        cell = table_ref[1, 0, slot] * 8 + table_ref[3, 0, slot]
        sum_ref[cell] = sum_ref[cell] + weight * inner
        return 0

    lax.fori_loop(0, 32, step, 0, unroll=16)
    norm = F32(0.0)
    for k in range(4):
        x = wave_ref[0, k].astype(F32)
        norm = norm + jnp.sum(x * x)
        for ri in range(8):
            mixed_ref[k, :, pl.ds(256 * ri, 256)] = sum_ref[k * 8 + ri].astype(BF16)
    norm_ref[...] = jnp.full((1, 128), norm, F32)


def first_right_kernel(order, late_ref, mixed_ref, right_ref, out_ref):
    pl.delay(late_ref[0, 0])

    right = right_ref[0].reshape(8 * 256, 256)
    for pair in range(0, 4, 2):
        mixed = mixed_ref[pl.ds(pair, 2)].reshape(2 * 256, 8 * 256)
        total = jnp.dot(mixed, right, preferred_element_type=F32)
        for k in range(2):
            for place, owner in enumerate(order):
                rows = total[256 * k + 16 * owner : 256 * k + 16 * owner + 16]
                out_ref[place, pl.ds(16 * (pair + k), 16), :] = rows.astype(BF16)


def sum_kernel(parts_ref, copies_ref):
    rows = parts_ref[0].astype(F32)
    for part in range(1, 16):
        rows = rows + parts_ref[part].astype(F32)
    first = rows.astype(BF16)
    for copy in range(16):
        copies_ref[copy] = first


def second_kernel(
    order,
    table_ref,
    coef_ref,
    count_ref,
    norm_ref,
    blocks_ref,
    wave_ref,
    left_ref,
    right_ref,
    out_ref,
    scale_ref,
    vector_ref,
    product_ref,
    total_ref,
):
    entries = 4 * 256 * 256
    overlap = jnp.zeros((16, 256), F32)
    for place, owner in enumerate(order):
        for k in range(4):
            first = blocks_ref[place, pl.ds(16 * k, 16), :].astype(F32)
            overlap = overlap + first * wave_ref[0, k, pl.ds(16 * owner, 16), :].astype(F32)
    rayleigh = jnp.sum(overlap) / entries / (jnp.max(norm_ref[...]) / entries + epsilon)
    square = jnp.zeros((16, 256), F32)
    for place, owner in enumerate(order):
        for k in range(4):
            first = blocks_ref[place, pl.ds(16 * k, 16), :].astype(F32)
            residual = first - rayleigh * wave_ref[0, k, pl.ds(16 * owner, 16), :].astype(F32)
            square = square + residual * residual
            vector_ref[k, pl.ds(16 * owner, 16), :] = residual.astype(BF16)
    left_products(left_ref, lambda src: vector_ref[src], product_ref)
    right_sums(table_ref, coef_ref, count_ref, product_ref, right_ref, total_ref)
    for k in range(4):
        for place, owner in enumerate(order):
            out_ref[place, pl.ds(16 * k, 16), :] = total_ref[k, pl.ds(16 * owner, 16), :].astype(BF16)
    scale_ref[...] = lax.rsqrt(jnp.full((1, 128), jnp.sum(square) / entries + epsilon, F32))


def scale_kernel(scale_ref, first_ref, parts_ref, first_out, out_ref):
    first_out[0] = first_ref[0].reshape(4, 16, 256)
    rows = parts_ref[0].astype(F32)
    for part in range(1, 16):
        rows = rows + parts_ref[part].astype(F32)
    scale = jnp.concatenate([scale_ref[...], scale_ref[...]], axis=1)
    out_ref[0] = (rows * scale).reshape(4, 16, 256).astype(BF16)


def params(mib):
    return pltpu.CompilerParams(vmem_limit_bytes=mib << 20)


ORDER = (0, 1, 3, 2, 4, 5, 7, 6, 8, 9, 11, 10, 12, 13, 15, 14)


def exchange(blocks):
    return lax.all_to_all(blocks, "term", 0, 0, axis_index_groups=[list(ORDER)])


def body(wavefunction, left_ops, right_ops, term_table, coefficients, term_counts):
    count = lax.axis_size("chain")
    right = lax.ppermute(right_ops, "chain", [(s, (s - 1) % count) for s in range(count)])
    chain = lax.axis_index("chain") % 16
    own = jnp.where(chain % 2 == 0, 7000, 0)
    for bond, wait in ((0, 0), (6, 0), (7, 5000), (14, 0), (15, 3500)):
        own = jnp.where(chain == bond, wait, own)
    late = own.reshape(1, 1).astype(jnp.int32)
    shape = jax.ShapeDtypeStruct
    table, coef, left, wave = pl.pallas_call(
        stage_kernel,
        out_shape=tuple(shape(a.shape, a.dtype) for a in (term_table, coefficients, left_ops, wavefunction)),
        in_specs=[HBM] * 4,
        out_specs=(VMEM,) * 4,
        scratch_shapes=[pltpu.SemaphoreType.DMA((4,))],
        compiler_params=params(4),
        name="stage",
    )(*(pltpu.with_memory_space_constraint(a, pltpu.HBM) for a in (term_table, coefficients, left_ops, wavefunction)))
    mixed, norm = pl.pallas_call(
        first_left_kernel,
        out_shape=(shape((4, 256, 2048), BF16), shape((1, 128), F32)),
        in_specs=[SMEM, SMEM, SMEM, VMEM, VMEM],
        out_specs=(VMEM, VMEM),
        scratch_shapes=[pltpu.VMEM((32, 256, 256), F32)],
        compiler_params=params(24),
        name="first_left",
    )(table, coef, term_counts, left, wave)
    partial = pl.pallas_call(
        functools.partial(first_right_kernel, ORDER),
        out_shape=shape((16, 64, 256), BF16),
        in_specs=[SMEM, VMEM, VMEM],
        out_specs=VMEM,
        compiler_params=params(16),
        name="first_right",
    )(late, mixed, right)
    copies = pl.pallas_call(
        sum_kernel,
        out_shape=shape((16, 64, 256), BF16),
        in_specs=[VMEM],
        out_specs=VMEM,
        compiler_params=params(8),
        name="sum",
    )(exchange(partial))
    partial, scale = pl.pallas_call(
        functools.partial(second_kernel, ORDER),
        out_shape=(shape((16, 64, 256), BF16), shape((1, 128), F32)),
        in_specs=[SMEM, SMEM, SMEM, VMEM, VMEM, VMEM, VMEM, VMEM],
        out_specs=(VMEM, VMEM),
        scratch_shapes=[
            pltpu.VMEM((4, 256, 256), BF16),
            pltpu.VMEM((4, 8, 256, 256), BF16),
            pltpu.VMEM((4, 256, 256), F32),
        ],
        compiler_params=params(16),
        name="second",
    )(table, coef, term_counts, norm, exchange(copies), wave, left, right)
    return pl.pallas_call(
        scale_kernel,
        out_shape=(shape((1, 4, 16, 256), BF16), shape((1, 4, 16, 256), BF16)),
        in_specs=[VMEM, VMEM, VMEM],
        out_specs=(VMEM, VMEM),
        compiler_params=params(8),
        name="scale",
    )(scale, copies, exchange(partial))


def solution(mesh):
    in_specs = (
        P("chain", None, None, None),
        P("chain", "term", None, None),
        P("chain", "term", None, None),
        P(None, "chain", "term"),
        P("chain", "term"),
        P("chain", "term"),
    )
    out_specs = (P("chain", None, "term", None), P("chain", None, "term", None))
    return jax.shard_map(body, mesh=mesh, in_specs=in_specs, out_specs=out_specs, check_vma=False)
```
